512 devices in a mesh: region: 8 (over z_hi, core), shard: 64 (over z_lo, x, y).
Axes of the slice: x: 4, y: 8, z: 8 (z_hi: 4, z_lo: 2; z = z_hi * 2 + z_lo), core: 2. Of those that a mesh axis runs over, the one named last changes fastest.
Arguments:
- points: bfloat16 [49152, 8, 128], P(('region', 'shard')), may hold values from -12 to 12
- block_owner: int32 [49152, 1], P(('region', 'shard')), may hold values from 0 to 63; in each aligned block of 96 rows (0 to 95, 96 to 191, ...) at most 3 rows name the same one
- block_node: int32 [49152], P(('region', 'shard')), may hold values from 0 to 1
- queries: bfloat16 [131072, 128], P(('region', 'shard')), may hold values from -240 to 240
- w_in: bfloat16 [128, 768], replicated, may hold values from -0.5 to 0.5
- w_key: bfloat16 [768, 768], replicated, may hold values from -0.21875 to 0.21875
- w_value: bfloat16 [768, 768], replicated, may hold values from -0.21875 to 0.21875
- w_query: bfloat16 [128, 768], replicated, may hold values from -0.5 to 0.5
- w_out: bfloat16 [768, 128], replicated, may hold values from -0.21875 to 0.21875
Outputs:
- readout: bfloat16 [131072, 128], P(('region', 'shard'))
The draws below stay inside these ranges and needn't reach their ends.
Inputs may be any that keep to these rules, and one draw needn't show every extreme that they name: `block_owner`: among the 96 blocks of one device no shard is named more than 3 times, and some device names one shard exactly 3 times.
All inputs are finite; a program needn't handle non-finite values.
Results may differ from the reference program's by a relative error of at most 0.018.
Values may be sent and summed in bfloat16 or wider, within the bound.
No kernel may reach another device: no remote copies, remote signals or barrier semaphores. Data moves between devices by JAX's collectives and lax.ppermute only.
A program may use at most 64 MiB of HBM per device.

```python
import math
import jax
import jax.numpy as jnp
import numpy as np
from jax import lax

D = 768
HEADS = 12
HEAD_DIM = 64
C_IN = 128
C_OUT = 128
BLK = 8
NB = 96
S_DEV = 2
Q_DEV = 256
SHARDS = 64
CAP = 3
BLOCKS = 49152
ANCHORS = 1024
QUERIES = 131072


def draw_points(key, part):
    base = jax.random.fold_in(key, 11)
    centre = jax.random.normal(jax.random.fold_in(base, 1), (BLOCKS, 1, C_IN), jnp.float32)
    jitter = jax.random.normal(jax.random.fold_in(base, 2), (BLOCKS, BLK, C_IN), jnp.float32)
    values = 1.5 * centre + 0.6 * jitter
    return jnp.clip(values, -12.0, 12.0).astype(jnp.bfloat16)


def draw_queries(key, part):
    base = jax.random.fold_in(key, 23)
    raw = jax.random.normal(jax.random.fold_in(base, 1), (QUERIES, C_IN), jnp.float32)
    values = raw
    return jnp.clip(values, -240.0, 240.0).astype(jnp.bfloat16)


def with_ends(entries, own_key, smallest, top_value):
    longest = entries.shape.index(max(entries.shape))
    spots = []
    for shift in (0, 1):
        where = [jax.random.randint(jax.random.fold_in(own_key, axis), (), 0, length) for axis, length in enumerate(entries.shape)]
        where[longest] = (where[longest] + shift) % entries.shape[longest]
        spots.append(tuple(where))
    return entries.at[spots[0]].set(smallest).at[spots[1]].set(top_value)


def deal_out(own_key, own, number, rows, amount, top, bound, skew):
    ranking = jax.random.permutation(own_key, amount)
    heavy_load, usual = shares(amount, rows * top, bound, skew, True), shares(amount, rows * top, bound, skew, False)
    places = jnp.arange(amount)

    def named(sizes, offset_by):
        used = int((sizes > 0).sum())
        fixed = max(1, used // 4)
        moved = fixed + (places - fixed + offset_by * (used - fixed)) % max(1, amount - fixed)
        return jnp.zeros((amount,), jnp.int32).at[ranking[jnp.where(places < fixed, places, moved)]].set(jnp.asarray(sizes, jnp.int32))

    sizes = jnp.where(number % 4 == 0, named(heavy_load, number // 4), named(usual, number - number // 4 - 1))
    mixed = jax.random.permutation(jax.random.fold_in(own, 3), amount)
    donor, receiver = mixed[0:amount // 2 * 2:2], mixed[1:amount // 2 * 2:2]
    slack = jnp.minimum(sizes[donor] - 1, bound - sizes[receiver]) // 2
    slack = jnp.where((donor == ranking[0]) | (receiver == ranking[0]) | (sizes[receiver] == 0), 0, jnp.maximum(slack, 0))
    moved = jax.random.randint(jax.random.fold_in(own, 4), (amount // 2,), 0, 1 << 20) % (slack + 1)
    sizes = sizes.at[donor].add(-moved).at[receiver].add(moved)
    labels = jnp.searchsorted(jnp.cumsum(sizes), jnp.arange(rows * top), side="right").astype(jnp.int32)
    grid = labels.reshape(top, rows).T
    grid = grid[jax.random.permutation(jax.random.fold_in(own, 1), rows)]
    offset_by = jax.random.randint(jax.random.fold_in(own, 2), (rows, 1), 0, top)
    return jnp.take_along_axis(grid, (jnp.arange(top)[None, :] + offset_by) % top, axis=1)


def shares(count, total, reach, skew, full):
    weights = [(1 << 20) // math.isqrt(standing ** skew) + 1 for standing in range(1, count + 1)]
    largest = reach if full else min(reach, max(-(-total // count), total * weights[0] // sum(weights)))
    least = 1 if total - largest >= count - 1 else 0
    counts, rest = [largest] + [least] * (count - 1), total - largest - least * (count - 1)
    while rest > 0:
        free = [i for i in range(1, count) if counts[i] < largest] or [i for i in range(1, count) if counts[i] < reach]
        pool, remaining = sum([weights[i] for i in free]), rest
        for i in free:
            more = min(reach - counts[i], max(1, remaining * weights[i] // pool), rest)
            counts[i] = counts[i] + more
            rest = rest - more
    return np.array(counts)


def noise(rng, extent, scale, most, kind=jnp.bfloat16):
    return jnp.clip(scale * jax.random.normal(rng, extent, jnp.float32), -most, most).astype(kind)


def setup_inputs(seed: int = 0) -> dict:
    arg_keys = jax.random.split(jax.random.key(seed), 10)
    points = draw_points(jax.random.fold_in(arg_keys[9], 71), 0)
    block_owner_keys = jax.random.split(jax.random.fold_in(arg_keys[1], 1), BLOCKS // NB)
    block_owner_turns = jax.random.permutation(jax.random.fold_in(arg_keys[1], 3), BLOCKS // NB)
    block_owner = jax.vmap(lambda own, number: deal_out(jax.random.fold_in(arg_keys[1], 2), own, number, NB, SHARDS, 1, CAP, 2))(block_owner_keys, block_owner_turns).reshape((BLOCKS, 1))
    block_node = with_ends(jax.random.randint(arg_keys[2], (BLOCKS,), 0, S_DEV), jax.random.fold_in(arg_keys[2], 1), 0, S_DEV - 1).astype(jnp.int32)
    queries = draw_queries(jax.random.fold_in(arg_keys[9], 71), 0)
    w_in = noise(arg_keys[4], (C_IN, D), C_IN ** -0.5, 0.5)
    w_key = noise(arg_keys[5], (D, D), D ** -0.5, 0.21875)
    w_value = noise(arg_keys[6], (D, D), D ** -0.5, 0.21875)
    w_query = noise(arg_keys[7], (C_IN, D), C_IN ** -0.5, 0.5)
    w_out = noise(arg_keys[8], (D, C_OUT), D ** -0.5, 0.21875)
    return {"points": points, "block_owner": block_owner, "block_node": block_node, "queries": queries, "w_in": w_in, "w_key": w_key, "w_value": w_value, "w_query": w_query, "w_out": w_out}


def layer_norm(pooled):
    mean = lax.optimization_barrier(jnp.mean(pooled, axis=-1, keepdims=True))
    centred = pooled - mean
    spread = lax.optimization_barrier(jnp.mean(centred * centred, axis=-1, keepdims=True))
    return (centred * lax.rsqrt(spread + 1e-05)).astype(jnp.bfloat16)

def reference(points, block_owner, block_node, queries, w_in, w_key, w_value, w_query, w_out):
    device_count = BLOCKS // NB
    region_of = jnp.arange(device_count, dtype=jnp.int32) // SHARDS
    grouped = points.reshape(device_count, NB, BLK, C_IN)
    owner_shard = block_owner[:, 0].reshape(device_count, NB)
    node_ids = ((region_of[:, None] * SHARDS + owner_shard) * S_DEV + block_node.reshape(device_count, NB)).astype(jnp.int32)

    def add_device(pooled, item):
        block_points, block_nodes = item
        message = jax.nn.gelu(jnp.einsum('bpc,cd->bpd', block_points.astype(jnp.float32), w_in.astype(jnp.float32))).astype(jnp.bfloat16)
        block_total = lax.optimization_barrier(jnp.sum(message.astype(jnp.float32), axis=1))
        return (pooled + jax.ops.segment_sum(block_total, block_nodes, num_segments=ANCHORS), None)
    pooled, unused = lax.scan(add_device, jnp.zeros((ANCHORS, D), jnp.float32), (grouped, node_ids))
    normed = layer_norm(pooled)
    keys = jnp.dot(normed, w_key, preferred_element_type=jnp.float32).astype(jnp.bfloat16)
    values = jnp.dot(normed, w_value, preferred_element_type=jnp.float32).astype(jnp.bfloat16)
    key_heads = keys.reshape(ANCHORS, HEADS, HEAD_DIM).astype(jnp.float32)
    value_heads = values.reshape(ANCHORS, HEADS, HEAD_DIM).astype(jnp.float32)
    score_scale = HEAD_DIM ** (-0.5)

    def attend_block(query_rows):
        query_vec = jnp.dot(query_rows, w_query, preferred_element_type=jnp.float32).astype(jnp.bfloat16)
        query_heads = query_vec.reshape(query_rows.shape[0], HEADS, HEAD_DIM).astype(jnp.float32)
        scores = jnp.einsum('qhd,ahd->qha', query_heads, key_heads) * score_scale
        expo = jnp.exp(scores - lax.optimization_barrier(jnp.max(scores, axis=-1, keepdims=True)))
        totals = lax.optimization_barrier(jnp.sum(expo, axis=-1))
        weights = expo.astype(jnp.bfloat16)
        summed = jnp.einsum('qha,ahd->qhd', weights.astype(jnp.float32), value_heads)
        attended = (summed / totals[..., None]).astype(jnp.bfloat16).reshape(query_rows.shape[0], D)
        return jnp.dot(attended, w_out, preferred_element_type=jnp.float32).astype(jnp.bfloat16)
    blocks_out = lax.map(attend_block, queries.reshape(device_count, Q_DEV, C_IN))
    return blocks_out.reshape(QUERIES, C_OUT)
```

```python
import functools

import jax
import jax.numpy as jnp
from jax import lax
from jax.experimental import pallas as pl
from jax.experimental.pallas import tpu as pltpu
from jax.sharding import Mesh
from jax.sharding import PartitionSpec as P

HEADS = 12
HEAD_DIM = 64
S_DEV = 2
AXES = ("z_hi", "core", "z_lo", "x", "y")
SHARD = ("z_lo", "x", "y")
BF16 = jnp.bfloat16
F32 = jnp.float32


def layer_norm(pooled):
    mean = jnp.mean(pooled, axis=-1, keepdims=True)
    centred = pooled - mean
    spread = jnp.mean(centred * centred, axis=-1, keepdims=True)
    return (centred * lax.rsqrt(spread + 1e-05)).astype(BF16)


def attention_kernel(queries, near, far, w_query, w_key, w_value, w_out, out, heads_out):
    group = 4 * HEAD_DIM
    anchors = (near[...], far[...])
    lane = lax.broadcasted_iota(jnp.int32, (1, group), 1) // HEAD_DIM
    for g in range(HEADS // 4):
        cols = slice(g * group, (g + 1) * group)
        q = jnp.dot(queries[...], w_query[:, cols], preferred_element_type=F32).astype(BF16)
        q = q * jnp.asarray(HEAD_DIM**-0.5, BF16)
        keys = [jnp.dot(a, w_key[:, cols], preferred_element_type=F32).astype(BF16) for a in anchors]
        values = [jnp.dot(a, w_value[:, cols], preferred_element_type=F32).astype(BF16) for a in anchors]
        result = jnp.zeros((q.shape[0], group), F32)
        for h in range(4):
            mine = lane == h
            q_head = jnp.where(mine, q, jnp.zeros_like(q))
            scores = [
                lax.dot_general(q_head, k, (((1,), (1,)), ((), ())), preferred_element_type=F32) for k in keys
            ]
            peak = jnp.maximum(
                jnp.max(scores[0], axis=-1, keepdims=True), jnp.max(scores[1], axis=-1, keepdims=True)
            )
            expo = [jnp.exp(s - peak) for s in scores]
            total = jnp.sum(expo[0], axis=-1, keepdims=True) + jnp.sum(expo[1], axis=-1, keepdims=True)
            summed = jnp.dot(expo[0].astype(BF16), values[0], preferred_element_type=F32)
            summed += jnp.dot(expo[1].astype(BF16), values[1], preferred_element_type=F32)
            result = jnp.where(mine, summed / total, result)
        heads_out[:, cols] = result.astype(BF16)
    out[...] = jnp.dot(heads_out[...], w_out[...], preferred_element_type=F32).astype(BF16)


def attention(queries, near, far, w_query, w_key, w_value, w_out):
    vmem = pl.BlockSpec(memory_space=pltpu.VMEM)
    return pl.pallas_call(
        attention_kernel,
        out_shape=jax.ShapeDtypeStruct((queries.shape[0], w_out.shape[1]), BF16),
        in_specs=[vmem] * 7,
        out_specs=vmem,
        scratch_shapes=[pltpu.VMEM((queries.shape[0], w_query.shape[1]), BF16)],
        compiler_params=pltpu.CompilerParams(vmem_limit_bytes=48 * 1024 * 1024),
        name="attention",
    )(queries, near, far, w_query, w_key, w_value, w_out)


def spread(rows, axes):
    count = lax.axis_size(axes)
    copies = jnp.broadcast_to(rows[None], (count, *rows.shape))
    return lax.all_to_all(copies, axes, 0, 0, tiled=True).reshape(-1, rows.shape[-1])


def body(points, block_owner, block_node, queries, w_in, w_key, w_value, w_query, w_out):
    shards = lax.axis_size(SHARD)
    block_count, block_points, in_features = points.shape
    width = w_in.shape[1]
    node = block_owner[:, 0] * S_DEV + block_node
    messages = jax.nn.gelu(
        jnp.dot(points.reshape(-1, in_features), w_in, preferred_element_type=F32)
    ).astype(BF16)
    pick = jnp.repeat(node, block_points)[None, :] == jnp.arange(shards * S_DEV, dtype=jnp.int32)[:, None]
    partial = jnp.dot(pick.astype(BF16), messages, preferred_element_type=F32).astype(BF16)
    arrived = lax.all_to_all(partial.reshape(shards, S_DEV, width), SHARD, 0, 0, tiled=True)
    normed = layer_norm(jnp.sum(arrived.astype(F32), axis=0))
    column = spread(normed, ("z_hi", "z_lo", "y"))
    near = spread(column, ("x",))
    far = lax.ppermute(near, "core", [(0, 1), (1, 0)])
    return attention(queries, near, far, w_query, w_key, w_value, w_out)


def solution(mesh):
    sizes = (mesh.shape["region"] // 2, 2, 2, 4, mesh.shape["shard"] // 8)
    fine = Mesh(mesh.devices.reshape(sizes), AXES)
    rows = P(AXES)
    return jax.shard_map(
        body,
        mesh=fine,
        in_specs=(rows, rows, rows, rows, P(), P(), P(), P(), P()),
        out_specs=rows,
        check_vma=False,
    )
```

```python
import functools

import jax
import jax.numpy as jnp
from jax import lax
from jax.experimental import pallas as pl
from jax.experimental.pallas import tpu as pltpu
from jax.sharding import Mesh
from jax.sharding import PartitionSpec as P

HEADS = 12
HEAD_DIM = 64
S_DEV = 2
GROUP = 4 * HEAD_DIM
AXES = ("z_hi", "core", "z_lo", "x", "y")
SHARD = ("z_lo", "x", "y")
BF16 = jnp.bfloat16
F32 = jnp.float32
VMEM = pl.BlockSpec(memory_space=pltpu.VMEM)
SMEM = pl.BlockSpec(memory_space=pltpu.SMEM)


def matmul(a, b, dims=((1,), (0,))):
    return lax.dot_general(a, b, (dims, ((), ())), preferred_element_type=F32)


def layer_norm(pooled):
    mean = jnp.mean(pooled, axis=-1, keepdims=True)
    centred = pooled - mean
    spread = jnp.mean(centred * centred, axis=-1, keepdims=True)
    return (centred * lax.rsqrt(spread + 1e-05)).astype(BF16)


def pool_kernel(block_points, owner, node, points, w_in, out, pick):
    blocks = owner.shape[0]
    rows = 2 * block_points
    slots = out.shape[0]
    lane = lax.broadcasted_iota(jnp.int32, (rows, slots), 1)
    first = lax.broadcasted_iota(jnp.int32, (rows, slots), 0) < block_points
    for pair in range(blocks // 2):
        ids = [owner[b] * S_DEV + node[b] for b in (2 * pair, 2 * pair + 1)]
        chosen = lane == jnp.where(first, ids[0], ids[1])
        pick[rows * pair : rows * (pair + 1), :] = jnp.where(chosen, 1.0, 0.0).astype(BF16)
    for g in range(w_in.shape[1] // GROUP):
        cols = slice(g * GROUP, (g + 1) * GROUP)
        messages = jax.nn.gelu(matmul(points[...], w_in[:, cols])).astype(BF16)
        out[:, cols] = matmul(pick[...], messages, ((0,), (0,))).astype(BF16)


def pool(points, owner, node, w_in, slots):
    blocks, block_points, features = points.shape
    rows = blocks * block_points
    return pl.pallas_call(
        functools.partial(pool_kernel, block_points),
        out_shape=jax.ShapeDtypeStruct((slots, w_in.shape[1]), BF16),
        in_specs=[SMEM, SMEM, VMEM, VMEM],
        out_specs=VMEM,
        scratch_shapes=[pltpu.VMEM((rows, slots), BF16)],
        compiler_params=pltpu.CompilerParams(vmem_limit_bytes=16 * 1024 * 1024),
        cost_estimate=pl.CostEstimate(flops=2**28, bytes_accessed=2**20, transcendentals=2**19),
        name="pool",
    )(owner, node, points.reshape(rows, features), w_in)


def attend(q, anchors, w_key, w_value, old, store):
    lane = lax.broadcasted_iota(jnp.int32, (1, GROUP), 1) // HEAD_DIM
    for g in range(HEADS // 4):
        cols = slice(g * GROUP, (g + 1) * GROUP)
        q_group = q[:, cols]
        keys = [matmul(a, w_key[:, cols]).astype(BF16) for a in anchors]
        values = [matmul(a, w_value[:, cols]).astype(BF16) for a in anchors]
        peaks, totals, shrinks, result = [], [], [], None
        for h in range(4):
            mine = lane == h
            q_head = jnp.where(mine, q_group, jnp.zeros_like(q_group))
            scores = [matmul(q_head, k, ((1,), (1,))) for k in keys]
            peak = functools.reduce(jnp.maximum, [jnp.max(s, axis=-1, keepdims=True) for s in scores])
            before = old(g * 4 + h)
            if before is not None:
                peak = jnp.maximum(peak, before[0])
            expo = [jnp.exp(s - peak) for s in scores]
            total = sum(jnp.sum(e, axis=-1, keepdims=True) for e in expo)
            summed = sum(matmul(e.astype(BF16), v) for e, v in zip(expo, values))
            if before is not None:
                shrink = jnp.exp(before[0] - peak)
                total = total + before[1] * shrink
                shrinks.append(shrink)
            peaks.append(peak)
            totals.append(total)
            result = summed if result is None else jnp.where(mine, summed, result)
        store(g, cols, peaks, totals, shrinks, result, lane)


def by_head(parts, lane):
    wide = jnp.broadcast_to(parts[0], (parts[0].shape[0], GROUP))
    for h in range(1, 4):
        wide = jnp.where(lane == h, parts[h], wide)
    return wide


def first_kernel(queries, w_query, own, other, w_key, w_value, q, stats, summed):
    q[...] = (matmul(queries[...], w_query[...]).astype(BF16)) * jnp.asarray(HEAD_DIM**-0.5, BF16)

    def store(g, cols, peaks, totals, shrinks, result, lane):
        for h in range(4):
            stats[:, g * 4 + h : g * 4 + h + 1] = peaks[h]
            stats[:, 64 + g * 4 + h : 64 + g * 4 + h + 1] = totals[h]
        summed[:, cols] = result

    attend(q, [own[...], other[...]], w_key, w_value, lambda head: None, store)


def picked(place, rows):
    return [rows[lax.rem(place[0] + i, rows.shape[0])] for i in range(1, rows.shape[0])]


def next_kernel(place, q, rows, w_key, w_value, stats, summed, new_stats, new_summed):
    def old(head):
        return stats[:, head : head + 1], stats[:, 64 + head : 65 + head]

    def store(g, cols, peaks, totals, shrinks, result, lane):
        for h in range(4):
            new_stats[:, g * 4 + h : g * 4 + h + 1] = peaks[h]
            new_stats[:, 64 + g * 4 + h : 64 + g * 4 + h + 1] = totals[h]
        new_summed[:, cols] = result + summed[:, cols] * by_head(shrinks, lane)

    attend(q, picked(place, rows), w_key, w_value, old, store)


def last_kernel(place, q, rows, w_key, w_value, stats, summed, w_out, out, heads_out):
    def old(head):
        return stats[:, head : head + 1], stats[:, 64 + head : 65 + head]

    def store(g, cols, peaks, totals, shrinks, result, lane):
        full = result + summed[:, cols] * by_head(shrinks, lane)
        heads_out[:, cols] = (full / by_head(totals, lane)).astype(BF16)

    attend(q, picked(place, rows), w_key, w_value, old, store)
    out[...] = matmul(heads_out[...], w_out[...]).astype(BF16)


def cost(queries, anchors):
    return pl.CostEstimate(
        flops=anchors * 768 * 768 * 4 + queries * anchors * 768 * 16,
        bytes_accessed=2**20,
        transcendentals=queries * anchors * HEADS,
    )


def spread(rows, axes):
    count = lax.axis_size(axes)
    copies = jnp.broadcast_to(rows[None], (count, *rows.shape))
    return lax.all_to_all(copies, axes, 0, 0, tiled=True)


def swap(rows):
    return lax.ppermute(rows, "core", [(0, 1), (1, 0)])


def attention(queries, column, w_query, w_key, w_value, w_out):
    count, width = queries.shape[0], w_query.shape[1]
    place = lax.axis_index("x").reshape(1)
    params = pltpu.CompilerParams(vmem_limit_bytes=20 * 1024 * 1024)
    state = [
        jax.ShapeDtypeStruct((count, 128), F32),
        jax.ShapeDtypeStruct((count, width), F32),
    ]
    near = spread(column, ("x",))
    other = swap(column)
    first = pl.pallas_call(
        first_kernel,
        out_shape=[jax.ShapeDtypeStruct((count, width), BF16), *state],
        in_specs=[VMEM] * 6,
        out_specs=[VMEM] * 3,
        compiler_params=params,
        cost_estimate=cost(count, 2 * column.shape[0]),
        name="attend_first",
    )(queries, w_query, column, other, w_key, w_value)
    q, stats, summed = first
    far = swap(near)
    stats, summed = pl.pallas_call(
        next_kernel,
        out_shape=state,
        in_specs=[SMEM] + [VMEM] * 6,
        out_specs=[VMEM] * 2,
        compiler_params=params,
        cost_estimate=cost(count, 3 * column.shape[0]),
        name="attend_next",
    )(place, q, near, w_key, w_value, stats, summed)
    return pl.pallas_call(
        last_kernel,
        out_shape=jax.ShapeDtypeStruct((count, w_out.shape[1]), BF16),
        in_specs=[SMEM] + [VMEM] * 7,
        out_specs=VMEM,
        scratch_shapes=[pltpu.VMEM((count, width), BF16)],
        compiler_params=params,
        cost_estimate=cost(count, 3 * column.shape[0]),
        name="attend_last",
    )(place, q, far, w_key, w_value, stats, summed, w_out)


def body(points, block_owner, block_node, queries, w_in, w_key, w_value, w_query, w_out):
    shards = lax.axis_size(SHARD)
    width = w_in.shape[1]
    partial = pool(points, block_owner[:, 0], block_node, w_in, shards * S_DEV)
    arrived = lax.all_to_all(partial.reshape(shards, S_DEV, width), SHARD, 0, 0, tiled=True)
    normed = layer_norm(jnp.sum(arrived.astype(F32), axis=0))
    column = spread(normed, ("z_hi", "z_lo", "y")).reshape(-1, width)
    return attention(queries, column, w_query, w_key, w_value, w_out)


def solution(mesh):
    sizes = (mesh.shape["region"] // 2, 2, 2, 4, mesh.shape["shard"] // 8)
    fine = Mesh(mesh.devices.reshape(sizes), AXES)
    rows = P(AXES)
    return jax.shard_map(
        body,
        mesh=fine,
        in_specs=(rows, rows, rows, rows, P(), P(), P(), P(), P()),
        out_specs=rows,
        check_vma=False,
    )
```

```python
import jax
import jax.numpy as jnp
from jax import lax
from jax.experimental import pallas as pl
from jax.experimental.pallas import tpu as pltpu
from jax.sharding import Mesh
from jax.sharding import PartitionSpec as P

HEADS = 12
HEAD_DIM = 64
S_DEV = 2
AXES = ("z_hi", "core", "z_lo", "x", "y")
SHARD = ("z_lo", "x", "y")
BF16 = jnp.bfloat16
F32 = jnp.float32
PAIR = 2 * HEAD_DIM
GROUP = 4 * HEAD_DIM
VMEM = pl.BlockSpec(memory_space=pltpu.VMEM)
NN, NT, TN = ((1,), (0,)), ((1,), (1,)), ((0,), (0,))


def layer_norm(pooled):
    mean = jnp.mean(pooled, axis=-1, keepdims=True)
    centred = pooled - mean
    spread = jnp.mean(centred * centred, axis=-1, keepdims=True)
    return (centred * lax.rsqrt(spread + 1e-05)).astype(BF16)


def matmul(a, b, dims=NN):
    return lax.dot_general(a, b, (dims, ((), ())), preferred_element_type=F32)


def attend(queries, w_query, rows, w_key, w_value, store):
    q_cols, keys, values, scores, weights = {}, {}, {}, {}, {}

    def project(g):
        cols = slice(g * GROUP, (g + 1) * GROUP)
        q = matmul(w_query[:, cols].T, queries[...], NT).astype(BF16)
        q_cols[g] = q * jnp.asarray(HEAD_DIM**-0.5, BF16)
        keys[g] = matmul(rows[...], w_key[:, cols]).astype(BF16)
        values[g] = matmul(rows[...], w_value[:, cols]).astype(BF16).T

    def score(head):
        g, h = head // 4, head % 4
        q = q_cols[g][h * HEAD_DIM : (h + 1) * HEAD_DIM]
        q = jnp.concatenate([q, jnp.zeros_like(q)] if h % 2 == 0 else [jnp.zeros_like(q), q], axis=0)
        scores[head] = matmul(keys[g][:, h // 2 * PAIR : (h // 2 + 1) * PAIR], q)

    def weigh(head):
        s = scores.pop(head)
        peak = jnp.max(s, axis=0, keepdims=True)
        expo = jnp.exp(s - peak)
        weights[head] = peak, jnp.sum(expo, axis=0, keepdims=True), expo.astype(BF16)

    def finish(head):
        peak, total, expo = weights.pop(head)
        mine = slice(head % 4 * HEAD_DIM, (head % 4 + 1) * HEAD_DIM)
        store(head, peak, total, matmul(values[head // 4][mine], expo))

    lead, tail, ahead = 2, 4, 2
    project(0)
    for step in range(HEADS + tail):
        if (step + ahead) % 4 == 0 and 0 < (step + ahead) // 4 < HEADS // 4:
            project((step + ahead) // 4)
        if step < HEADS:
            score(step)
        if lead <= step < HEADS + lead:
            weigh(step - lead)
        if step >= tail:
            finish(step - tail)


def near_kernel(queries, w_query, rows, w_key, w_value, stats, summed):
    def store(head, peak, total, result):
        stats[head : head + 1, :] = peak
        stats[16 + head : 17 + head, :] = total
        summed[head * HEAD_DIM : (head + 1) * HEAD_DIM, :] = result

    attend(queries, w_query, rows, w_key, w_value, store)


def far_kernel(queries, w_query, rows, w_key, w_value, stats, summed, w_out, out, heads):
    def store(head, peak, total, result):
        mine = slice(head * HEAD_DIM, (head + 1) * HEAD_DIM)
        before = stats[head : head + 1, :]
        top = jnp.maximum(before, peak)
        old, new = jnp.exp(before - top), jnp.exp(peak - top)
        whole = stats[16 + head : 17 + head, :] * old + total * new
        heads[mine, :] = ((summed[mine, :] * old + result * new) / whole).astype(BF16)

    attend(queries, w_query, rows, w_key, w_value, store)
    out[...] = matmul(heads[...], w_out[...], TN).astype(BF16)


def attention(queries, near, w_query, w_key, w_value, w_out):
    count, width = queries.shape[0], w_query.shape[1]
    anchors = near.shape[0]
    how = dict(
        compiler_params=pltpu.CompilerParams(vmem_limit_bytes=16 * 1024 * 1024),
        cost_estimate=pl.CostEstimate(
            flops=anchors * width * (width * 4 + count * 16),
            bytes_accessed=2**20,
            transcendentals=count * anchors * HEADS,
        ),
    )
    far = lax.ppermute(near, "core", [(0, 1), (1, 0)])
    stats, summed = pl.pallas_call(
        near_kernel,
        out_shape=[jax.ShapeDtypeStruct((32, count), F32), jax.ShapeDtypeStruct((width, count), F32)],
        in_specs=[VMEM] * 5,
        out_specs=[VMEM] * 2,
        name="near",
        **how,
    )(queries, w_query, near, w_key, w_value)
    return pl.pallas_call(
        far_kernel,
        out_shape=jax.ShapeDtypeStruct((count, w_out.shape[1]), BF16),
        in_specs=[VMEM] * 8,
        out_specs=VMEM,
        scratch_shapes=[pltpu.VMEM((width, count), BF16)],
        name="far",
        **how,
    )(queries, w_query, far, w_key, w_value, stats, summed, w_out)


def spread(rows, axes):
    count = lax.axis_size(axes)
    copies = jnp.broadcast_to(rows[None], (count, *rows.shape))
    return lax.all_to_all(copies, axes, 0, 0, tiled=True).reshape(-1, rows.shape[-1])


def body(points, block_owner, block_node, queries, w_in, w_key, w_value, w_query, w_out):
    shards = lax.axis_size(SHARD)
    _, block_points, in_features = points.shape
    width = w_in.shape[1]
    node = block_owner[:, 0] * S_DEV + block_node
    messages = jax.nn.gelu(
        jnp.dot(points.reshape(-1, in_features), w_in, preferred_element_type=F32)
    ).astype(BF16)
    pick = jnp.repeat(node, block_points)[None, :] == jnp.arange(shards * S_DEV, dtype=jnp.int32)[:, None]
    partial = jnp.dot(pick.astype(BF16), messages, preferred_element_type=F32).astype(BF16)
    arrived = lax.all_to_all(partial.reshape(shards, S_DEV, width), SHARD, 0, 0, tiled=True)
    normed = layer_norm(jnp.sum(arrived.astype(F32), axis=0))
    column = spread(normed, ("z_hi", "z_lo", "y"))
    near = spread(column, ("x",))
    return attention(queries, near, w_query, w_key, w_value, w_out)


def solution(mesh):
    sizes = (mesh.shape["region"] // 2, 2, 2, 4, mesh.shape["shard"] // 8)
    fine = Mesh(mesh.devices.reshape(sizes), AXES)
    rows = P(AXES)
    return jax.shard_map(
        body,
        mesh=fine,
        in_specs=(rows, rows, rows, rows, P(), P(), P(), P(), P()),
        out_specs=rows,
        check_vma=False,
    )
```

```python
import functools
import math

import jax
import jax.numpy as jnp
from jax import lax
from jax.experimental import pallas as pl
from jax.experimental.pallas import tpu as pltpu
from jax.sharding import Mesh
from jax.sharding import PartitionSpec as P

HEADS = 12
HEAD_DIM = 64
S_DEV = 2
GELU_A = 2 * (2 / math.pi) ** 0.5
GELU_B = 4 * 0.044715 * GELU_A
AXES = ("z_hi", "core", "z_lo", "x", "y")
SHARD = ("z_lo", "x", "y")
BF16 = jnp.bfloat16
F32 = jnp.float32
PAIR = 2 * HEAD_DIM
GROUP = 4 * HEAD_DIM
VMEM = pl.BlockSpec(memory_space=pltpu.VMEM)
HBM = pl.BlockSpec(memory_space=pltpu.HBM)
NN, NT, TN = ((1,), (0,)), ((1,), (1,)), ((0,), (0,))


def layer_norm(pooled):
    mean = jnp.mean(pooled, axis=-1, keepdims=True)
    centred = pooled - mean
    spread = jnp.mean(centred * centred, axis=-1, keepdims=True)
    return (centred * lax.rsqrt(spread + 1e-05)).astype(BF16)


def matmul(a, b, dims=NN):
    return lax.dot_general(a, b, (dims, ((), ())), preferred_element_type=F32)


def pool_kernel(block_points, owner_in, node_in, points_in, w_in_in, out, owner, node, points, w_in, pick, sems):
    pairs = ((owner_in, owner), (node_in, node), (w_in_in, w_in), (points_in, points))
    copies = [pltpu.make_async_copy(a, b, sems.at[i]) for i, (a, b) in enumerate(pairs)]
    for copy in copies:
        copy.start()
    blocks, slots = owner.shape[0], pick.shape[1]
    rows = 2 * block_points
    lane = lax.broadcasted_iota(jnp.int32, (rows, slots), 1)
    first = lax.broadcasted_iota(jnp.int32, (rows, slots), 0) < block_points
    copies[0].wait()
    copies[1].wait()
    for pair in range(blocks // 2):
        ids = [owner[b] * S_DEV + node[b] for b in (2 * pair, 2 * pair + 1)]
        chosen = lane == jnp.where(first, ids[0], ids[1])
        pick[rows * pair : rows * (pair + 1), :] = jnp.where(chosen, 1.0, 0.0).astype(BF16)
    copies[2].wait()
    copies[3].wait()
    messages = {}
    groups = w_in.shape[1] // GROUP

    def send(g):
        half = matmul(points[...], w_in[:, g * GROUP : (g + 1) * GROUP]) * 0.5
        inner = half * (GELU_A + GELU_B * (half * half))
        messages[g] = (half + half * jnp.tanh(inner)).astype(BF16)

    def gather(g):
        pooled = matmul(pick[...], messages.pop(g), TN).astype(BF16)
        cols = slice(g * GROUP, (g + 1) * GROUP)
        out[:, :, cols] = pooled.reshape(out.shape[0], out.shape[1], GROUP)

    for g in range(groups + 1):
        if g < groups:
            send(g)
        if g > 0:
            gather(g - 1)


def pool(points, owner, node, w_in, slots):
    blocks, block_points, features = points.shape
    rows = blocks * block_points
    return pl.pallas_call(
        functools.partial(pool_kernel, block_points),
        out_shape=jax.ShapeDtypeStruct((slots // S_DEV, S_DEV, w_in.shape[1]), BF16),
        in_specs=[HBM] * 4,
        out_specs=VMEM,
        scratch_shapes=[
            pltpu.SMEM((blocks,), jnp.int32),
            pltpu.SMEM((blocks,), jnp.int32),
            pltpu.VMEM((rows, features), BF16),
            pltpu.VMEM(w_in.shape, BF16),
            pltpu.VMEM((rows, slots), BF16),
            pltpu.SemaphoreType.DMA((4,)),
        ],
        compiler_params=pltpu.CompilerParams(vmem_limit_bytes=60 * 1024 * 1024),
        cost_estimate=pl.CostEstimate(flops=2**28, bytes_accessed=2**20, transcendentals=2**19),
        name="pool",
    )(owner, node, points.reshape(rows, features), w_in)


def attend(queries, w_query, rows, w_key, w_value, store, tail, ahead):
    q_cols, keys, values, scores, weights = {}, {}, {}, {}, {}

    def project(g):
        cols = slice(g * GROUP, (g + 1) * GROUP)
        q = matmul(w_query[:, cols].T, queries[...], NT).astype(BF16)
        q_cols[g] = q * jnp.asarray(HEAD_DIM**-0.5, BF16)
        keys[g] = matmul(rows[...], w_key[:, cols]).astype(BF16)
        values[g] = matmul(rows[...], w_value[:, cols]).astype(BF16).T

    def score(head):
        g, h = head // 4, head % 4
        q = q_cols[g][h * HEAD_DIM : (h + 1) * HEAD_DIM]
        q = jnp.concatenate([q, jnp.zeros_like(q)] if h % 2 == 0 else [jnp.zeros_like(q), q], axis=0)
        scores[head] = matmul(keys[g][:, h // 2 * PAIR : (h // 2 + 1) * PAIR], q)

    def weigh(head):
        s = scores.pop(head)
        peak = jnp.max(s, axis=0, keepdims=True)
        expo = jnp.exp(s - peak)
        weights[head] = peak, jnp.sum(expo, axis=0, keepdims=True), expo.astype(BF16)

    def finish(head):
        peak, total, expo = weights.pop(head)
        mine = slice(head % 4 * HEAD_DIM, (head % 4 + 1) * HEAD_DIM)
        store(head, peak, total, matmul(values[head // 4][mine], expo))

    lead = tail - 2
    project(0)
    for step in range(HEADS + tail):
        if (step + ahead) % 4 == 0 and 0 < (step + ahead) // 4 < HEADS // 4:
            project((step + ahead) // 4)
        if step < HEADS:
            score(step)
        if lead <= step < HEADS + lead:
            weigh(step - lead)
        if step >= tail:
            finish(step - tail)


def near_kernel(queries, w_query, rows, w_key, w_value, stats, summed):
    def store(head, peak, total, result):
        stats[head : head + 1, :] = peak
        stats[16 + head : 17 + head, :] = total
        summed[head * HEAD_DIM : (head + 1) * HEAD_DIM, :] = result

    attend(queries, w_query, rows, w_key, w_value, store, 4, 3)


def far_kernel(queries, w_query, rows, w_key, w_value, stats, summed, w_out, out, heads):
    def store(head, peak, total, result):
        mine = slice(head * HEAD_DIM, (head + 1) * HEAD_DIM)
        before = stats[head : head + 1, :]
        top = jnp.maximum(before, peak)
        old, new = jnp.exp(before - top), jnp.exp(peak - top)
        share = 1.0 / (stats[16 + head : 17 + head, :] * old + total * new)
        heads[mine, :] = (summed[mine, :] * (old * share) + result * (new * share)).astype(BF16)

    attend(queries, w_query, rows, w_key, w_value, store, 5, 2)
    out[...] = matmul(heads[...], w_out[...], TN).astype(BF16)


def attention(queries, near, w_query, w_key, w_value, w_out):
    count, width = queries.shape[0], w_query.shape[1]
    anchors = near.shape[0]
    how = dict(
        compiler_params=pltpu.CompilerParams(vmem_limit_bytes=16 * 1024 * 1024),
        cost_estimate=pl.CostEstimate(
            flops=anchors * width * (width * 4 + count * 16),
            bytes_accessed=2**20,
            transcendentals=count * anchors * HEADS,
        ),
    )
    far = lax.ppermute(near, "core", [(0, 1), (1, 0)])
    stats, summed = pl.pallas_call(
        near_kernel,
        out_shape=[jax.ShapeDtypeStruct((32, count), F32), jax.ShapeDtypeStruct((width, count), F32)],
        in_specs=[VMEM] * 5,
        out_specs=[VMEM] * 2,
        name="near",
        **how,
    )(queries, w_query, near, w_key, w_value)
    return pl.pallas_call(
        far_kernel,
        out_shape=jax.ShapeDtypeStruct((count, w_out.shape[1]), BF16),
        in_specs=[VMEM] * 8,
        out_specs=VMEM,
        scratch_shapes=[pltpu.VMEM((width, count), BF16)],
        name="far",
        **how,
    )(queries, w_query, far, w_key, w_value, stats, summed, w_out)


def norm_kernel(arrived, out):
    normed = layer_norm(jnp.sum(arrived[...].astype(F32), axis=0))
    out[...] = jnp.broadcast_to(normed[None], out.shape)


def normed_copies(arrived, axes):
    return pl.pallas_call(
        norm_kernel,
        out_shape=jax.ShapeDtypeStruct((lax.axis_size(axes), *arrived.shape[1:]), BF16),
        in_specs=[VMEM],
        out_specs=VMEM,
        compiler_params=pltpu.CompilerParams(vmem_limit_bytes=16 * 1024 * 1024),
        name="norm",
    )(arrived)


def spread(rows, axes):
    count = lax.axis_size(axes)
    copies = jnp.broadcast_to(rows[None], (count, *rows.shape))
    return lax.all_to_all(copies, axes, 0, 0, tiled=True).reshape(-1, rows.shape[-1])


def body(points, block_owner, block_node, queries, w_in, w_key, w_value, w_query, w_out):
    shards = lax.axis_size(SHARD)
    width = w_in.shape[1]
    partial = pool(points, block_owner[:, 0], block_node, w_in, shards * S_DEV)
    arrived = lax.all_to_all(partial.reshape(shards, S_DEV, width), SHARD, 0, 0, tiled=True)
    copies = normed_copies(arrived, ("z_hi", "z_lo", "y"))
    column = lax.all_to_all(copies, ("z_hi", "z_lo", "y"), 0, 0, tiled=True).reshape(-1, width)
    near = spread(column, ("x",))
    return attention(queries, near, w_query, w_key, w_value, w_out)


def solution(mesh):
    sizes = (mesh.shape["region"] // 2, 2, 2, 4, mesh.shape["shard"] // 8)
    fine = Mesh(mesh.devices.reshape(sizes), AXES)
    rows = P(AXES)
    return jax.shard_map(
        body,
        mesh=fine,
        in_specs=(rows, rows, rows, rows, P(), P(), P(), P(), P()),
        out_specs=rows,
        check_vma=False,
    )
```

```python
import functools
import math

import jax
import jax.numpy as jnp
from jax import lax
from jax.experimental import pallas as pl
from jax.experimental.pallas import tpu as pltpu
from jax.sharding import Mesh
from jax.sharding import PartitionSpec as P

HEADS = 12
HEAD_DIM = 64
S_DEV = 2
GELU_A = 2 * (2 / math.pi) ** 0.5
GELU_B = 4 * 0.044715 * GELU_A
AXES = ("z_hi", "core", "z_lo", "x", "y")
SHARD = ("z_lo", "x", "y")
BF16 = jnp.bfloat16
F32 = jnp.float32
PAIR = 2 * HEAD_DIM
GROUP = 4 * HEAD_DIM
VMEM = pl.BlockSpec(memory_space=pltpu.VMEM)
HBM = pl.BlockSpec(memory_space=pltpu.HBM)
NN, NT, TN = ((1,), (0,)), ((1,), (1,)), ((0,), (0,))


def layer_norm(pooled):
    mean = jnp.mean(pooled, axis=-1, keepdims=True)
    centred = pooled - mean
    spread = jnp.mean(centred * centred, axis=-1, keepdims=True)
    return (centred * lax.rsqrt(spread + 1e-05)).astype(BF16)


def matmul(a, b, dims=NN):
    return lax.dot_general(a, b, (dims, ((), ())), preferred_element_type=F32)


def pool_kernel(block_points, owner_in, node_in, points_in, w_in_in, out, owner, node, points, w_in, pick, sems):
    pairs = ((owner_in, owner), (node_in, node), (w_in_in, w_in), (points_in, points))
    copies = [pltpu.make_async_copy(a, b, sems.at[i]) for i, (a, b) in enumerate(pairs)]
    for copy in copies:
        copy.start()
    blocks, slots = owner.shape[0], pick.shape[1]
    rows = 2 * block_points
    lane = lax.broadcasted_iota(jnp.int32, (rows, slots), 1)
    first = lax.broadcasted_iota(jnp.int32, (rows, slots), 0) < block_points
    copies[0].wait()
    copies[1].wait()
    for pair in range(blocks // 2):
        ids = [owner[b] * S_DEV + node[b] for b in (2 * pair, 2 * pair + 1)]
        chosen = lane == jnp.where(first, ids[0], ids[1])
        pick[rows * pair : rows * (pair + 1), :] = jnp.where(chosen, 1.0, 0.0).astype(BF16)
    copies[2].wait()
    w_in[...] = w_in[...] * jnp.asarray(0.5, BF16)
    copies[3].wait()
    messages = {}
    groups = w_in.shape[1] // 256

    def send(g):
        half = matmul(points[...], w_in[:, g * 256 : (g + 1) * 256])
        inner = half * (GELU_A + GELU_B * (half * half))
        messages[g] = (half + half * jnp.tanh(inner)).astype(BF16)

    def gather(g):
        pooled = matmul(pick[...], messages.pop(g), TN).astype(BF16)
        cols = slice(g * 256, (g + 1) * 256)
        out[:, :, cols] = pooled.reshape(out.shape[0], out.shape[1], 256)

    for g in range(groups + 1):
        if g < groups:
            send(g)
        if g > 0:
            gather(g - 1)


def pool(points, owner, node, w_in, slots):
    blocks, block_points, features = points.shape
    rows = blocks * block_points
    return pl.pallas_call(
        functools.partial(pool_kernel, block_points),
        out_shape=jax.ShapeDtypeStruct((slots // S_DEV, S_DEV, w_in.shape[1]), BF16),
        in_specs=[HBM] * 4,
        out_specs=VMEM,
        scratch_shapes=[
            pltpu.SMEM((blocks,), jnp.int32),
            pltpu.SMEM((blocks,), jnp.int32),
            pltpu.VMEM((rows, features), BF16),
            pltpu.VMEM(w_in.shape, BF16),
            pltpu.VMEM((rows, slots), BF16),
            pltpu.SemaphoreType.DMA((4,)),
        ],
        compiler_params=pltpu.CompilerParams(
            vmem_limit_bytes=60 * 1024 * 1024
        ),
        cost_estimate=pl.CostEstimate(flops=2**28, bytes_accessed=2**20, transcendentals=2**19),
        name="pool",
    )(owner, node, points.reshape(rows, features), w_in)


def attend(q_cols, keys_of, values_of, store, tail, ahead):
    keys, values, scores, weights = {}, {}, {}, {}

    def project(g):
        keys[g], values[g] = keys_of(g), values_of(g)

    def score(head):
        g, h = head // 4, head % 4
        q = q_cols[head * HEAD_DIM : (head + 1) * HEAD_DIM, :]
        q = jnp.concatenate([q, jnp.zeros_like(q)] if h % 2 == 0 else [jnp.zeros_like(q), q], axis=0)
        scores[head] = matmul(keys[g][:, h // 2 * PAIR : (h // 2 + 1) * PAIR], q)

    def weigh(head):
        s = scores.pop(head)
        peak = jnp.max(s, axis=0, keepdims=True)
        expo = jnp.exp(s - peak)
        weights[head] = peak, jnp.sum(expo, axis=0, keepdims=True), expo.astype(BF16)

    def finish(head):
        peak, total, expo = weights.pop(head)
        mine = slice(head % 4 * HEAD_DIM, (head % 4 + 1) * HEAD_DIM)
        store(head, peak, total, matmul(values[head // 4][mine], expo))

    lead = tail - 2
    project(0)
    for step in range(HEADS + tail):
        if (step + ahead) % 4 == 0 and 0 < (step + ahead) // 4 < HEADS // 4:
            project((step + ahead) // 4)
        if step < HEADS:
            score(step)
        if lead <= step < HEADS + lead:
            weigh(step - lead)
        if step >= tail:
            finish(step - tail)


def query_kernel(queries, other_queries, w_query, own, other):
    turned = w_query[...].T
    for source, target in ((queries, own), (other_queries, other)):
        target[...] = matmul(turned, source[...], NT).astype(BF16) * jnp.asarray(HEAD_DIM**-0.5, BF16)


def give_kernel(q_cols, rows, w_key, w_value, keys, values, given):
    def keys_of(g):
        cols = slice(g * GROUP, (g + 1) * GROUP)
        part = matmul(rows[...], w_key[:, cols]).astype(BF16)
        keys[:, cols] = part
        return part

    def values_of(g):
        cols = slice(g * GROUP, (g + 1) * GROUP)
        part = matmul(rows[...], w_value[:, cols]).astype(BF16).T
        values[cols, :] = part
        return part

    width = values.shape[0]
    gathered = []

    def store(head, peak, total, result):
        given[head * HEAD_DIM : (head + 1) * HEAD_DIM, :] = result.astype(BF16)
        gathered.append((peak, total))
        if head == HEADS - 1:
            rest = jnp.concatenate([p for p, _ in gathered] + [t for _, t in gathered], axis=0)
            for term in range(3):
                part = rest.astype(BF16)
                at = width + 32 * term
                given[at : at + 2 * HEADS, :] = part
                given[at + 2 * HEADS : at + 32, :] = jnp.zeros((32 - 2 * HEADS, part.shape[1]), BF16)
                rest = rest - part.astype(F32)

    attend(q_cols, keys_of, values_of, store, 4, 3)


def own_kernel(q_cols, keys, values, stats, summed):
    def store(head, peak, total, result):
        stats[head : head + 1, :] = peak
        stats[HEADS + head : HEADS + head + 1, :] = total
        summed[head * HEAD_DIM : (head + 1) * HEAD_DIM, :] = result

    def keys_of(g):
        return keys[:, g * GROUP : (g + 1) * GROUP]

    def values_of(g):
        return values[g * GROUP : (g + 1) * GROUP, :]

    attend(q_cols, keys_of, values_of, store, 4, 3)


def merge_kernel(stats, summed, given, w_out, out, heads):
    width = summed.shape[0]
    terms = [given[width + 32 * t : width + 32 * t + 2 * HEADS, :].astype(F32) for t in range(3)]
    other = (terms[2] + terms[1]) + terms[0]
    peaks, totals = (stats[:HEADS, :], other[:HEADS]), (stats[HEADS : 2 * HEADS, :], other[HEADS:])
    top = jnp.maximum(*peaks)
    old, new = jnp.exp(peaks[0] - top), jnp.exp(peaks[1] - top)
    share = 1.0 / (totals[0] * old + totals[1] * new)
    old, new = old * share, new * share
    for head in range(HEADS):
        mine = slice(head * HEAD_DIM, (head + 1) * HEAD_DIM)
        both = summed[mine, :] * old[head : head + 1] + given[mine, :].astype(F32) * new[head : head + 1]
        heads[mine, :] = both.astype(BF16)
    out[...] = matmul(heads[...], w_out[...], TN).astype(BF16)


def call(kernel, shapes, operands, scratch=(), flops=0, exps=0):
    return pl.pallas_call(
        kernel,
        out_shape=shapes,
        in_specs=[VMEM] * len(operands),
        out_specs=[VMEM] * len(shapes),
        scratch_shapes=list(scratch),
        compiler_params=pltpu.CompilerParams(vmem_limit_bytes=16 * 1024 * 1024),
        cost_estimate=pl.CostEstimate(flops=flops, bytes_accessed=2**20, transcendentals=exps),
    )(*operands)


def swap(rows):
    return lax.ppermute(rows, "core", [(0, 1), (1, 0)])


def attention(q_own, q_other, near, w_key, w_value, w_out):
    width, count = q_own.shape
    anchors = near.shape[0]
    flops, exps = anchors * width * count * 16, count * anchors * HEADS
    keys, values, given = call(
        give_kernel,
        [
            jax.ShapeDtypeStruct((anchors, width), BF16),
            jax.ShapeDtypeStruct((width, anchors), BF16),
            jax.ShapeDtypeStruct((width + 96, count), BF16),
        ],
        (q_other, near, w_key, w_value),
        flops=flops * 2,
        exps=exps,
    )
    given = swap(given)
    stats, summed = call(
        own_kernel,
        [jax.ShapeDtypeStruct((2 * HEADS, count), F32), jax.ShapeDtypeStruct((width, count), F32)],
        (q_own, keys, values),
        flops=flops,
        exps=exps,
    )
    return call(
        merge_kernel,
        [jax.ShapeDtypeStruct((count, w_out.shape[1]), BF16)],
        (stats, summed, given, w_out),
        scratch=[pltpu.VMEM((width, count), BF16)],
    )[0]


def norm_kernel(arrived, out):
    normed = layer_norm(jnp.sum(arrived[...].astype(F32), axis=0))
    out[...] = jnp.broadcast_to(normed[None], out.shape)


def normed_copies(arrived, axes):
    return pl.pallas_call(
        norm_kernel,
        out_shape=jax.ShapeDtypeStruct((lax.axis_size(axes), *arrived.shape[1:]), BF16),
        in_specs=[VMEM],
        out_specs=VMEM,
        compiler_params=pltpu.CompilerParams(vmem_limit_bytes=16 * 1024 * 1024),
        name="norm",
    )(arrived)


def spread(rows, axes):
    count = lax.axis_size(axes)
    copies = jnp.broadcast_to(rows[None], (count, *rows.shape))
    return lax.all_to_all(copies, axes, 0, 0, tiled=True).reshape(-1, rows.shape[-1])


def body(points, block_owner, block_node, queries, w_in, w_key, w_value, w_query, w_out):
    shards = lax.axis_size(SHARD)
    width = w_in.shape[1]
    partial = pool(points, block_owner[:, 0], block_node, w_in, shards * S_DEV)
    arrived = lax.all_to_all(partial.reshape(shards, S_DEV, width), SHARD, 0, 0, tiled=True)
    other_queries = swap(queries)
    shape = jax.ShapeDtypeStruct((width, queries.shape[0]), BF16)
    q_own, q_other = call(query_kernel, [shape, shape], (queries, other_queries, w_query), flops=2**27)
    copies = normed_copies(arrived, ("z_hi", "z_lo", "y"))
    column = lax.all_to_all(copies, ("z_hi", "z_lo", "y"), 0, 0, tiled=True).reshape(-1, width)
    near = spread(column, ("x",)).reshape(-1, width)
    return attention(q_own, q_other, near, w_key, w_value, w_out)


def solution(mesh):
    sizes = (mesh.shape["region"] // 2, 2, 2, 4, mesh.shape["shard"] // 8)
    fine = Mesh(mesh.devices.reshape(sizes), AXES)
    rows = P(AXES)
    return jax.shard_map(
        body,
        mesh=fine,
        in_specs=(rows, rows, rows, rows, P(), P(), P(), P(), P()),
        out_specs=rows,
        check_vma=False,
    )
```

```python
import functools
import math

import jax
import jax.numpy as jnp
from jax import lax
from jax.experimental import pallas as pl
from jax.experimental.pallas import tpu as pltpu
from jax.sharding import Mesh
from jax.sharding import PartitionSpec as P

HEADS = 12
HEAD_DIM = 64
S_DEV = 2
GELU_A = 2 * (2 / math.pi) ** 0.5
GELU_B = 4 * 0.044715 * GELU_A
AXES = ("z_hi", "core", "z_lo", "x", "y")
SHARD = ("z_lo", "x", "y")
EXCHANGE = ("x", "z_lo", "y")
COLUMN = ("z_lo", "y", "z_hi")
BF16 = jnp.bfloat16
F32 = jnp.float32
PAIR = 2 * HEAD_DIM
GROUP = 4 * HEAD_DIM
VMEM = pl.BlockSpec(memory_space=pltpu.VMEM)
HBM = pl.BlockSpec(memory_space=pltpu.HBM)
NN, NT, TN = ((1,), (0,)), ((1,), (1,)), ((0,), (0,))


def layer_norm(pooled):
    mean = jnp.mean(pooled, axis=-1, keepdims=True)
    centred = pooled - mean
    spread = jnp.mean(centred * centred, axis=-1, keepdims=True)
    return (centred * lax.rsqrt(spread + 1e-05)).astype(BF16)


def matmul(a, b, dims=NN):
    return lax.dot_general(a, b, (dims, ((), ())), preferred_element_type=F32)


def pool_kernel(block_points, sizes, owner_in, node_in, points_in, w_in_in, out, owner, node, points, w_in, pick, sems):
    pairs = ((owner_in, owner), (node_in, node), (w_in_in, w_in), (points_in, points))
    copies = [pltpu.make_async_copy(a, b, sems.at[i]) for i, (a, b) in enumerate(pairs)]
    for copy in copies:
        copy.start()
    blocks, slots = owner.shape[0], pick.shape[1]
    rows = 2 * block_points
    lane = lax.broadcasted_iota(jnp.int32, (rows, slots), 1)
    place, lane = lane // S_DEV, lane % S_DEV
    for axis in reversed(EXCHANGE):
        later = SHARD[SHARD.index(axis) + 1 :]
        lane = lane + place % sizes[axis] * (S_DEV * math.prod(sizes[a] for a in later))
        place = place // sizes[axis]
    first = lax.broadcasted_iota(jnp.int32, (rows, slots), 0) < block_points
    copies[0].wait()
    copies[1].wait()
    for pair in range(blocks // 2):
        ids = [owner[b] * S_DEV + node[b] for b in (2 * pair, 2 * pair + 1)]
        chosen = lane == jnp.where(first, ids[0], ids[1])
        pick[rows * pair : rows * (pair + 1), :] = jnp.where(chosen, 1.0, 0.0).astype(BF16)
    copies[2].wait()
    w_in[...] = w_in[...] * jnp.asarray(0.5, BF16)
    copies[3].wait()
    messages = {}
    groups = w_in.shape[1] // 256

    def send(g):
        half = matmul(points[...], w_in[:, g * 256 : (g + 1) * 256])
        inner = half * (GELU_A + GELU_B * (half * half))
        messages[g] = (half + half * jnp.tanh(inner)).astype(BF16)

    def gather(g):
        pooled = matmul(pick[...], messages.pop(g), TN).astype(BF16)
        cols = slice(g * 256, (g + 1) * 256)
        out[:, :, cols] = pooled.reshape(out.shape[0], out.shape[1], 256)

    for g in range(groups + 1):
        if g < groups:
            send(g)
        if g > 0:
            gather(g - 1)


def pool(points, owner, node, w_in, slots):
    blocks, block_points, features = points.shape
    rows = blocks * block_points
    return pl.pallas_call(
        functools.partial(pool_kernel, block_points, {a: lax.axis_size(a) for a in SHARD}),
        out_shape=jax.ShapeDtypeStruct((slots // S_DEV, S_DEV, w_in.shape[1]), BF16),
        in_specs=[HBM] * 4,
        out_specs=VMEM,
        scratch_shapes=[
            pltpu.SMEM((blocks,), jnp.int32),
            pltpu.SMEM((blocks,), jnp.int32),
            pltpu.VMEM((rows, features), BF16),
            pltpu.VMEM(w_in.shape, BF16),
            pltpu.VMEM((rows, slots), BF16),
            pltpu.SemaphoreType.DMA((4,)),
        ],
        compiler_params=pltpu.CompilerParams(
            vmem_limit_bytes=60 * 1024 * 1024
        ),
        cost_estimate=pl.CostEstimate(flops=2**28, bytes_accessed=2**20, transcendentals=2**19),
        name="pool",
    )(owner, node, points.reshape(rows, features), w_in)


def attend(q_cols, keys_of, values_of, store, tail, ahead):
    keys, values, scores, weights = {}, {}, {}, {}

    def project(g):
        keys[g], values[g] = keys_of(g), values_of(g)

    def score(head):
        g, h = head // 4, head % 4
        q = q_cols[head * HEAD_DIM : (head + 1) * HEAD_DIM, :]
        q = jnp.concatenate([q, jnp.zeros_like(q)] if h % 2 == 0 else [jnp.zeros_like(q), q], axis=0)
        scores[head] = matmul(keys[g][:, h // 2 * PAIR : (h // 2 + 1) * PAIR], q)

    def weigh(head):
        s = scores.pop(head)
        peak = jnp.max(s, axis=0, keepdims=True)
        expo = jnp.exp(s - peak)
        weights[head] = peak, jnp.sum(expo, axis=0, keepdims=True), expo.astype(BF16)

    def finish(head):
        peak, total, expo = weights.pop(head)
        mine = slice(head % 4 * HEAD_DIM, (head % 4 + 1) * HEAD_DIM)
        store(head, peak, total, matmul(values[head // 4][mine], expo))

    lead = tail - 2
    project(0)
    for step in range(HEADS + tail):
        if (step + ahead) % 4 == 0 and 0 < (step + ahead) // 4 < HEADS // 4:
            project((step + ahead) // 4)
        if step < HEADS:
            score(step)
        if lead <= step < HEADS + lead:
            weigh(step - lead)
        if step >= tail:
            finish(step - tail)


def query_kernel(queries, other_queries, w_query, own, other):
    turned = w_query[...].T
    for source, target in ((queries, own), (other_queries, other)):
        target[...] = matmul(turned, source[...], NT).astype(BF16) * jnp.asarray(HEAD_DIM**-0.5, BF16)


def give_kernel(q_cols, rows, w_key, w_value, keys, values, given):
    def keys_of(g):
        cols = slice(g * GROUP, (g + 1) * GROUP)
        part = matmul(rows[...], w_key[:, cols]).astype(BF16)
        keys[:, cols] = part
        return part

    def values_of(g):
        cols = slice(g * GROUP, (g + 1) * GROUP)
        part = matmul(rows[...], w_value[:, cols]).astype(BF16).T
        values[cols, :] = part
        return part

    width = values.shape[0]
    gathered = []

    def store(head, peak, total, result):
        given[head * HEAD_DIM : (head + 1) * HEAD_DIM, :] = result.astype(BF16)
        gathered.append((peak, total))
        if head == HEADS - 1:
            rest = jnp.concatenate([p for p, _ in gathered] + [t for _, t in gathered], axis=0)
            for term in range(3):
                part = rest.astype(BF16)
                at = width + 32 * term
                given[at : at + 2 * HEADS, :] = part
                given[at + 2 * HEADS : at + 32, :] = jnp.zeros((32 - 2 * HEADS, part.shape[1]), BF16)
                rest = rest - part.astype(F32)

    attend(q_cols, keys_of, values_of, store, 4, 3)


def own_kernel(q_cols, keys, values, stats, summed):
    def store(head, peak, total, result):
        stats[head : head + 1, :] = peak
        stats[HEADS + head : HEADS + head + 1, :] = total
        summed[head * HEAD_DIM : (head + 1) * HEAD_DIM, :] = result

    def keys_of(g):
        return keys[:, g * GROUP : (g + 1) * GROUP]

    def values_of(g):
        return values[g * GROUP : (g + 1) * GROUP, :]

    attend(q_cols, keys_of, values_of, store, 4, 3)


def merge_kernel(stats, summed, given, w_out, out, heads):
    width = summed.shape[0]
    terms = [given[width + 32 * t : width + 32 * t + 2 * HEADS, :].astype(F32) for t in range(3)]
    other = (terms[2] + terms[1]) + terms[0]
    peaks, totals = (stats[:HEADS, :], other[:HEADS]), (stats[HEADS : 2 * HEADS, :], other[HEADS:])
    top = jnp.maximum(*peaks)
    old, new = jnp.exp(peaks[0] - top), jnp.exp(peaks[1] - top)
    share = 1.0 / (totals[0] * old + totals[1] * new)
    old, new = old * share, new * share
    for head in range(HEADS):
        mine = slice(head * HEAD_DIM, (head + 1) * HEAD_DIM)
        both = summed[mine, :] * old[head : head + 1] + given[mine, :].astype(F32) * new[head : head + 1]
        heads[mine, :] = both.astype(BF16)
    out[...] = matmul(heads[...], w_out[...], TN).astype(BF16)


def call(kernel, shapes, operands, scratch=(), flops=0, exps=0):
    return pl.pallas_call(
        kernel,
        out_shape=shapes,
        in_specs=[VMEM] * len(operands),
        out_specs=[VMEM] * len(shapes),
        scratch_shapes=list(scratch),
        compiler_params=pltpu.CompilerParams(vmem_limit_bytes=16 * 1024 * 1024),
        cost_estimate=pl.CostEstimate(flops=flops, bytes_accessed=2**20, transcendentals=exps),
    )(*operands)


def swap(rows):
    return lax.ppermute(rows, "core", [(0, 1), (1, 0)])


def attention(q_own, q_other, near, w_key, w_value, w_out):
    width, count = q_own.shape
    anchors = near.shape[0]
    flops, exps = anchors * width * count * 16, count * anchors * HEADS
    keys, values, given = call(
        give_kernel,
        [
            jax.ShapeDtypeStruct((anchors, width), BF16),
            jax.ShapeDtypeStruct((width, anchors), BF16),
            jax.ShapeDtypeStruct((width + 96, count), BF16),
        ],
        (q_other, near, w_key, w_value),
        flops=flops * 2,
        exps=exps,
    )
    given = swap(given)
    stats, summed = call(
        own_kernel,
        [jax.ShapeDtypeStruct((2 * HEADS, count), F32), jax.ShapeDtypeStruct((width, count), F32)],
        (q_own, keys, values),
        flops=flops,
        exps=exps,
    )
    return call(
        merge_kernel,
        [jax.ShapeDtypeStruct((count, w_out.shape[1]), BF16)],
        (stats, summed, given, w_out),
        scratch=[pltpu.VMEM((width, count), BF16)],
    )[0]


def norm_kernel(arrived, out):
    normed = layer_norm(jnp.sum(arrived[...].astype(F32), axis=0))
    out[...] = jnp.broadcast_to(normed[None], out.shape)


def normed_copies(arrived, axes):
    return pl.pallas_call(
        norm_kernel,
        out_shape=jax.ShapeDtypeStruct((lax.axis_size(axes), *arrived.shape[1:]), BF16),
        in_specs=[VMEM],
        out_specs=VMEM,
        compiler_params=pltpu.CompilerParams(vmem_limit_bytes=16 * 1024 * 1024),
        name="norm",
    )(arrived)


def spread(rows, axes):
    count = lax.axis_size(axes)
    copies = jnp.broadcast_to(rows[None], (count, *rows.shape))
    return lax.all_to_all(copies, axes, 0, 0, tiled=True).reshape(-1, rows.shape[-1])


def body(points, block_owner, block_node, queries, w_in, w_key, w_value, w_query, w_out):
    shards = lax.axis_size(SHARD)
    width = w_in.shape[1]
    partial = pool(points, block_owner[:, 0], block_node, w_in, shards * S_DEV)
    arrived = lax.all_to_all(partial.reshape(shards, S_DEV, width), EXCHANGE, 0, 0, tiled=True)
    other_queries = swap(queries)
    shape = jax.ShapeDtypeStruct((width, queries.shape[0]), BF16)
    q_own, q_other = call(query_kernel, [shape, shape], (queries, other_queries, w_query), flops=2**27)
    copies = normed_copies(arrived, COLUMN)
    column = lax.all_to_all(copies, COLUMN, 0, 0, tiled=True).reshape(-1, width)
    near = spread(column, ("x",)).reshape(-1, width)
    return attention(q_own, q_other, near, w_key, w_value, w_out)


def solution(mesh):
    sizes = (mesh.shape["region"] // 2, 2, 2, 4, mesh.shape["shard"] // 8)
    fine = Mesh(mesh.devices.reshape(sizes), AXES)
    rows = P(AXES)
    return jax.shard_map(
        body,
        mesh=fine,
        in_specs=(rows, rows, rows, rows, P(), P(), P(), P(), P()),
        out_specs=rows,
        check_vma=False,
    )
```
